32 devices in a mesh: dp: 16 (over z, y, core), tensor: 2 (over x).
Axes of the slice: x: 2, y: 2, z: 4, core: 2. Of those that a mesh axis runs over, the one named last changes fastest.
Arguments:
- queries: bfloat16 [8192, 4096], P(('dp', 'tensor')), may hold values from -6 to 6
- key_rows: bfloat16 [8192, 512], P(('dp', 'tensor')), may hold values from -6 to 6
- value_rows: bfloat16 [8192, 512], P(('dp', 'tensor')), may hold values from -150 to 150
- norm_gain: float32 [4096], replicated, may hold values from 0.1 to 1.9
- labels: int32 [8192], P('dp'), may hold values from 0 to 12, as said below
- pair_list: int32 [16, 2], replicated, may hold values from 0 to 11, as said below
- owner_map: int32 [16], replicated, may hold values from 0 to 15, each once
Outputs:
- gram: bfloat16 [16, 4096, 4096], P('dp', 'tensor')
- harvest: bfloat16 [8192, 4096], P('dp', 'tensor')
The draws below stay inside these ranges and needn't reach their ends.
Inputs may be any that keep to these rules, and one draw needn't show every extreme that they name: Class 12 marks a token without a class. Among the 512 tokens of one sequence every class 0 to 11 labels 1 to 12 tokens, and one class of the first listed pair labels exactly 12 tokens in every sequence. `pair_list`: 16 different pairs, the first class below the second.
All inputs are finite; a program needn't handle non-finite values.
Results may differ from the reference program's by a relative error of at most 0.0056.
Values may be sent and summed in bfloat16 or wider, within the bound.
No kernel may reach another device: no remote copies, remote signals or barrier semaphores. Data moves between devices by JAX's collectives and lax.ppermute only.
A program may use at most 128 MiB of HBM per device.

```python
import math
import jax
import jax.numpy as jnp
import numpy as np
from jax import lax

H = 32
KVH = 4
HD = 128
D = 4096
C = 12
P_SIZE = 16
SLOT = 12
SEQ = 512
TOKENS = 8192
NQ = 1
GR = 4096
N_DP = 16


def choose_pairs(key):
    firsts, seconds = np.triu_indices(C, 1)
    table = jnp.asarray(np.stack([firsts, seconds], axis=1).astype(np.int32))
    order = jax.random.permutation(jax.random.fold_in(key, 41), table.shape[0])
    return table[order[:P_SIZE]]


def draw_queries(key, part):
    shape = (TOKENS, H, HD)
    values = jnp.clip(jax.random.normal(jax.random.fold_in(key, 1), shape, jnp.float32), -4.0, 4.0)
    return values.reshape(TOKENS, H * HD).astype(jnp.bfloat16)


def draw_key_rows(key, part):
    shape = (TOKENS, KVH, HD)
    values = jnp.clip(jax.random.normal(jax.random.fold_in(key, 2), shape, jnp.float32), -4.0, 4.0)
    return values.reshape(TOKENS, KVH * HD).astype(jnp.bfloat16)


def draw_value_rows(key, part):
    shape = (TOKENS, KVH, HD)
    values = jnp.clip(jax.random.normal(jax.random.fold_in(key, 3), shape, jnp.float32), -4.0, 4.0)
    head_factor = 1.0 + 2.0 * jnp.arange(KVH, dtype=jnp.float32) / max(KVH - 1, 1)
    column = head_factor[:, None] * jnp.exp(jax.random.uniform(jax.random.fold_in(key, 4), (KVH, HD), jnp.float32) * math.log(4.0))
    row_scale = jnp.exp(jax.random.uniform(jax.random.fold_in(key, 5), (TOKENS,), jnp.float32) * math.log(3.0))
    values = values * row_scale[:, None, None] * column[None, :, :]
    return values.reshape(TOKENS, KVH * HD).astype(jnp.bfloat16)


def draw_pair_list(key, part):
    return choose_pairs(key)


def draw_labels(key, part):
    pairs = choose_pairs(key)
    full_class = pairs[0, 0]
    group_total = TOKENS // SEQ

    def one_group(group_index):
        group_key = jax.random.fold_in(jax.random.fold_in(key, 43), group_index)
        ceiling = 1 + (SLOT - 1) * group_index // max(group_total - 1, 1)
        counts = jax.random.randint(jax.random.fold_in(group_key, 1), (C,), 1, ceiling + 1)
        counts = jnp.where(jnp.arange(C) == full_class, SLOT, counts).astype(jnp.int32)
        bounds = jnp.cumsum(counts)
        order = jax.random.permutation(jax.random.fold_in(group_key, 2), SEQ)
        rank_of = jnp.zeros((SEQ,), jnp.int32).at[order].set(jnp.arange(SEQ, dtype=jnp.int32))
        return jnp.sum((rank_of[:, None] >= bounds[None, :]).astype(jnp.int32), axis=1).astype(jnp.int32)
    return jax.vmap(one_group)(jnp.arange(group_total, dtype=jnp.int32)).reshape(TOKENS)


def setup_inputs(seed: int = 0) -> dict:
    arg_keys = jax.random.split(jax.random.key(seed), 8)
    return {
        "queries": draw_queries(jax.random.fold_in(arg_keys[7], 71), 0),
        "key_rows": draw_key_rows(jax.random.fold_in(arg_keys[7], 71), 0),
        "value_rows": draw_value_rows(jax.random.fold_in(arg_keys[7], 71), 0),
        "norm_gain": jnp.clip(1.0 + 0.18 * jax.random.normal(arg_keys[3], (D,), jnp.float32), 0.1, 1.9),
        "labels": draw_labels(jax.random.fold_in(arg_keys[7], 71), 0),
        "pair_list": draw_pair_list(jax.random.fold_in(arg_keys[7], 71), 0),
        "owner_map": jax.random.permutation(arg_keys[6], N_DP).astype(jnp.int32),
    }


NEGATIVE = -1e+30
EPSILON = 1e-06

def attend_group(query_group, key_group, value_group):
    seq_len = query_group.shape[0]
    group_size = H // KVH
    block_rows = min(seq_len, 512)
    score_scale = 1.0 / math.sqrt(HD)
    query_full = query_group.astype(jnp.float32).reshape(seq_len, KVH, group_size, HD)
    key_full = key_group.astype(jnp.float32).reshape(seq_len, KVH, HD)
    value_full = value_group.astype(jnp.float32).reshape(seq_len, KVH, HD)
    pieces_out = []
    for block_start in range(0, seq_len, block_rows):
        block_end = block_start + block_rows
        scores = jnp.einsum('skgd,nkd->kgsn', query_full[block_start:block_end], key_full[:block_end]) * score_scale
        allowed = jnp.arange(block_end)[None, :] <= (block_start + jnp.arange(block_rows))[:, None]
        scores = jnp.where(allowed, scores, NEGATIVE)
        row_max = lax.optimization_barrier(jnp.max(scores, axis=-1, keepdims=True))
        expo_vals = jnp.where(allowed, jnp.exp(scores - row_max), 0.0)
        row_total = lax.optimization_barrier(jnp.sum(expo_vals, axis=-1))
        weights = lax.optimization_barrier(expo_vals.astype(jnp.bfloat16)).astype(jnp.float32)
        mixed_out = jnp.einsum('kgsn,nkd->skgd', weights, value_full[:block_end])
        pieces_out.append(mixed_out / jnp.transpose(row_total, (2, 0, 1))[:, :, :, None])
    return jnp.concatenate(pieces_out, axis=0).reshape(seq_len, H * HD)

def class_rows(harvest, labels, class_count, slot_count):
    seq_len = labels.shape[0]
    onehot = (labels[:, None] == jnp.arange(class_count, dtype=jnp.int32)[None, :]).astype(jnp.int32)
    ranks = jnp.cumsum(onehot, axis=0) - onehot
    picked = onehot[None, :, :] * (ranks[None, :, :] == jnp.arange(slot_count, dtype=jnp.int32)[:, None, None]).astype(jnp.int32)
    positions = lax.optimization_barrier(jnp.sum(picked * jnp.arange(seq_len, dtype=jnp.int32)[None, :, None], axis=1))
    present = lax.optimization_barrier(jnp.sum(picked, axis=1))
    gathered = harvest[jnp.transpose(positions)]
    return gathered * jnp.transpose(present)[:, :, None].astype(harvest.dtype)

def reference(queries, key_rows, value_rows, norm_gain, labels, pair_list, owner_map):
    query_groups = queries.reshape(N_DP, SEQ, H * HD)
    key_groups = key_rows.reshape(N_DP, SEQ, KVH * HD)
    value_groups = value_rows.reshape(N_DP, SEQ, KVH * HD)
    label_groups = labels.reshape(N_DP, SEQ)

    def per_group(inputs):
        query_group, key_group, value_group, label_group = inputs
        attended = attend_group(query_group, key_group, value_group)
        meansq = lax.optimization_barrier(jnp.mean(attended * attended, axis=1))
        harvest = (attended * lax.rsqrt(meansq + EPSILON)[:, None] * norm_gain[None, :]).astype(jnp.bfloat16)
        selected = class_rows(harvest, label_group, C, SLOT)
        onehot = (label_group[:, None] == jnp.arange(C, dtype=jnp.int32)[None, :]).astype(jnp.float32)
        return (selected, lax.optimization_barrier(jnp.sum(onehot, axis=0)), harvest)
    selected, group_counts, harvests = lax.map(per_group, (query_groups, key_groups, value_groups, label_groups))
    count = lax.optimization_barrier(jnp.sum(group_counts, axis=0))
    by_class = jnp.transpose(selected, (1, 0, 2, 3)).reshape(C, N_DP * SLOT, D)

    def gram_of(class_block):
        return jnp.dot(jnp.transpose(class_block), class_block, preferred_element_type=jnp.float32)
    class_grams = lax.map(gram_of, by_class)

    def owner_tile(block_id):
        pair = pair_list[block_id // NQ]
        share = (block_id % NQ).astype(jnp.int32)
        both = class_grams[pair[0]] + class_grams[pair[1]]
        columns = lax.dynamic_slice_in_dim(both, share * GR, GR, 1)
        return (columns / (count[pair[0]] + count[pair[1]])).astype(jnp.bfloat16)
    return (lax.map(owner_tile, owner_map), harvests.reshape(TOKENS, D))
```

```python
import math

import jax
import jax.numpy as jnp
from jax import lax
from jax.experimental import pallas as pl
from jax.experimental.pallas import tpu as pltpu
from jax.sharding import PartitionSpec as P

H = 32
KVH = 4
HD = 128
D = 4096
C = 12
P_SIZE = 16
SLOT = 12


NEGATIVE = -1e30
EPSILON = 1e-06

BF16 = jnp.bfloat16
F32 = jnp.float32


def from_root(shard, axis, root):
    mine = lax.axis_index(axis) == root
    return lax.psum(jnp.where(mine, shard, jnp.zeros_like(shard)), axis)


def folded_keys(query_heads, key_heads, value_heads, offset, block_rows):
    local_rows, head_count, head_width = query_heads.shape
    kv_count = key_heads.shape[1]
    group_size = head_count // kv_count
    score_scale = 1.0 / math.sqrt(head_width)
    grouped = query_heads.reshape(local_rows, kv_count, group_size, head_width)
    positions = offset + jnp.arange(local_rows)
    initial = (
        jnp.full((kv_count, group_size, local_rows), NEGATIVE, jnp.float32),
        jnp.zeros((kv_count, group_size, local_rows), jnp.float32),
        jnp.zeros((kv_count, group_size, local_rows, head_width), jnp.float32),
    )
    pieces = (
        lax.all_gather(key_heads, "tensor", axis=0, tiled=True),
        lax.all_gather(value_heads, "tensor", axis=0, tiled=True),
    )
    piece_start = jnp.int32(0)

    def compute(state_in):
        row_max, row_total, accumulated = state_in
        key_piece, value_piece = pieces
        piece_rows = key_piece.shape[0]
        for sub_start in range(0, piece_rows, block_rows):
            key_block = key_piece[sub_start : sub_start + block_rows]
            value_block = value_piece[sub_start : sub_start + block_rows]
            span_rows = key_block.shape[0]
            scores = (
                jnp.einsum("skgd,nkd->kgsn", grouped, key_block, preferred_element_type=jnp.float32)
                * score_scale
            )
            key_places = piece_start + sub_start + jnp.arange(span_rows)
            allowed = key_places[None, :] <= positions[:, None]
            scores = jnp.where(allowed, scores, NEGATIVE)
            new_max = jnp.maximum(row_max, jnp.max(scores, axis=-1))
            expo_vals = jnp.where(allowed, jnp.exp(scores - new_max[..., None]), 0.0)
            factor = jnp.exp(row_max - new_max)
            row_total = row_total * factor + jnp.sum(expo_vals, axis=-1)
            accumulated = accumulated * factor[..., None] + jnp.einsum(
                "kgsn,nkd->kgsd",
                expo_vals.astype(jnp.bfloat16),
                value_block,
                preferred_element_type=jnp.float32,
            )
            row_max = new_max
        return (row_max, row_total, accumulated)

    row_max, row_total, accumulated = lax.cond(
        piece_start <= offset + local_rows - 1, compute, lambda state_in: state_in, initial
    )
    attended = accumulated / row_total[..., None]
    return jnp.transpose(attended, (2, 0, 1, 3)).reshape(local_rows, head_count * head_width)


def class_rows(harvest, labels, class_count, slot_count):
    seq_len = labels.shape[0]
    onehot = (labels[:, None] == jnp.arange(class_count, dtype=jnp.int32)[None, :]).astype(
        jnp.int32
    )
    ranks = jnp.cumsum(onehot, axis=0) - onehot
    picked = onehot[None, :, :] * (
        ranks[None, :, :] == jnp.arange(slot_count, dtype=jnp.int32)[:, None, None]
    ).astype(jnp.int32)
    positions = jnp.sum(picked * jnp.arange(seq_len, dtype=jnp.int32)[None, :, None], axis=1)
    present = jnp.sum(picked, axis=1)
    gathered = harvest[jnp.transpose(positions)]
    return gathered * jnp.transpose(present)[:, :, None].astype(harvest.dtype)


def general_local(queries, key_rows, value_rows, norm_gain, labels, pair_list, owner_map):
    tensor_count = lax.axis_size("tensor")
    group_count = lax.axis_size("dp")
    local_rows = queries.shape[0]
    seq_len = local_rows * tensor_count
    block_rows = min(seq_len, 512)
    part_width = D // tensor_count
    my_tensor = lax.axis_index("tensor")
    my_group = lax.axis_index("dp")
    query_heads = queries.reshape(local_rows, H, HD)
    key_heads = key_rows.reshape(local_rows, KVH, HD)
    value_heads = value_rows.reshape(local_rows, KVH, HD)
    attended = folded_keys(query_heads, key_heads, value_heads, my_tensor * local_rows, block_rows)
    squares = jnp.sum(attended * attended, axis=1)
    whole_rows = (attended * lax.rsqrt(squares / D + EPSILON)[:, None] * norm_gain[None, :]).astype(
        jnp.bfloat16
    )
    harvest = lax.all_to_all(whole_rows, "tensor", split_axis=1, concat_axis=0, tiled=True)
    class_ids = jnp.arange(C, dtype=jnp.int32)
    local_counts = jnp.sum((labels[:, None] == class_ids[None, :]).astype(jnp.float32), axis=0)
    counts = lax.psum(local_counts, "dp")
    per_class = class_rows(harvest, labels, C, SLOT)
    blocks_per_pair = group_count // P_SIZE
    dest_classes = pair_list[owner_map // blocks_per_pair]
    outgoing = per_class[dest_classes]
    incoming = lax.all_to_all(outgoing, "dp", split_axis=0, concat_axis=0, tiled=True)
    stacked = incoming.reshape(-1, part_width)
    my_block = owner_map[my_group]
    my_classes = pair_list[my_block // blocks_per_pair]
    my_share = my_block % blocks_per_pair
    pair_count = counts[my_classes[0]] + counts[my_classes[1]]
    slice_count = P_SIZE * tensor_count // group_count
    received = []
    for slot_index in range(slice_count):
        received.append(from_root(stacked, "tensor", my_share * slice_count + slot_index))
    chosen = jnp.concatenate(received, axis=1)
    tile = lax.dot_general(
        stacked, chosen, (((0,), (0,)), ((), ())), preferred_element_type=jnp.float32
    )
    return ((tile / pair_count).astype(jnp.bfloat16)[None], harvest)


BLOCKS = 8
ROWS = 2 * SLOT
EXTRA = HD
VMEM_SPEC = pl.BlockSpec(memory_space=pltpu.VMEM)


def cost(flops, moved, exps=0):
    return pl.CostEstimate(flops=flops, bytes_accessed=moved, transcendentals=exps)


def nt(left, right):
    return lax.dot_general(left, right, (((1,), (1,)), ((), ())), preferred_element_type=F32)


def dot(left, right):
    return lax.dot_general(left, right, (((1,), (0,)), ((), ())), preferred_element_type=F32)


def attend_heads(q_ref, kd, vd, ko, vo, use_off, put):
    rows = q_ref.shape[0]
    heads = q_ref.shape[1] // HD
    factor = math.log2(math.e) / math.sqrt(HD)

    def run(with_off):
        row = lax.broadcasted_iota(jnp.int32, (rows, rows), 0)
        col = lax.broadcasted_iota(jnp.int32, (rows, rows), 1)
        allowed = col <= row
        for head in range(heads):
            query = q_ref[:, head * HD : (head + 1) * HD]
            diag = jnp.where(allowed, nt(query, kd[...]), NEGATIVE)
            peak = jnp.max(diag, axis=-1, keepdims=True)
            if with_off:
                off = nt(query, ko[...])
                peak = jnp.maximum(peak, jnp.max(off, axis=-1, keepdims=True))
            diag_w = jnp.exp2((diag - peak) * factor)
            total = jnp.sum(diag_w, axis=-1, keepdims=True)
            mixed = dot(diag_w.astype(BF16), vd[...])
            if with_off:
                off_w = jnp.exp2((off - peak) * factor)
                total = total + jnp.sum(off_w, axis=-1, keepdims=True)
                mixed = mixed + dot(off_w.astype(BF16), vo[...])
            put(head, mixed * (1.0 / total))

    @pl.when(use_off)
    def _():
        run(True)

    @pl.when(jnp.logical_not(use_off))
    def _():
        run(False)


def own_kernel(place, q_ref, k_ref, v_ref, kp_ref, vp_ref, att_ref, sq_ref):
    sq_ref[...] = jnp.zeros_like(sq_ref)

    def put(head, value):
        att_ref[:, head * HD : (head + 1) * HD] = value
        sq_ref[0] += value * value

    attend_heads(q_ref, k_ref, v_ref, kp_ref, vp_ref, place[0] == 1, put)


def attend_own(place, queries, key_rows, value_rows, partner_kv):
    rows = queries.shape[0]
    wide = D // KVH
    return pl.pallas_call(
        own_kernel,
        grid_spec=pltpu.PrefetchScalarGridSpec(
            num_scalar_prefetch=1,
            grid=(2,),
            in_specs=[
                pl.BlockSpec((rows, wide), lambda i, t: (0, 2 * t[0] + i)),
                pl.BlockSpec((rows, HD), lambda i, t: (0, 2 * t[0] + i)),
                pl.BlockSpec((rows, HD), lambda i, t: (0, 2 * t[0] + i)),
                pl.BlockSpec((rows, HD), lambda i, t: (0, i)),
                pl.BlockSpec((rows, HD), lambda i, t: (0, 2 + i)),
            ],
            out_specs=[
                pl.BlockSpec((rows, wide), lambda i, t: (0, i)),
                pl.BlockSpec((1, rows, HD), lambda i, t: (i, 0, 0)),
            ],
        ),
        out_shape=[
            jax.ShapeDtypeStruct((rows, 2 * wide), F32),
            jax.ShapeDtypeStruct((2, rows, HD), F32),
        ],
        cost_estimate=cost(2 * 2 * 16 * rows * 2 * rows * HD, 4 << 20, 16 * rows * 2 * rows),
        name="attend_own",
    )(place, queries, key_rows, value_rows, partner_kv, partner_kv)


def partner_a_kernel(
    place, q_ref, kd, vd, ko, vo, own_ref, so_ref, sp_ref, att_ref, sq_ref, out_ref
):
    sq_ref[...] = jnp.zeros_like(sq_ref)

    def put(head, value):
        att_ref[:, head * HD : (head + 1) * HD] = value
        sq_ref[...] += value * value

    attend_heads(q_ref, kd, vd, ko, vo, place[0] == 0, put)
    picked = dot(so_ref[...], own_ref[...].astype(BF16))
    out_ref[...] = (picked + dot(sp_ref[...], att_ref[...].astype(BF16))).astype(BF16)


def partner_specs(rows, wide, chunk):
    return [
        pl.BlockSpec((rows, wide), lambda i, t: (0, 0)),
        pl.BlockSpec((rows, HD), lambda i, t: (0, chunk)),
        pl.BlockSpec((rows, HD), lambda i, t: (0, 2 + chunk)),
        pl.BlockSpec((rows, HD), lambda i, t: (0, 2 * t[0] + chunk)),
        pl.BlockSpec((rows, HD), lambda i, t: (0, 2 * t[0] + chunk)),
    ]


def attend_partner_a(place, query_a, partner_kv, key_rows, value_rows, att_own, picks):
    rows, wide = query_a.shape
    out_rows = picks.shape[0]
    return pl.pallas_call(
        partner_a_kernel,
        grid_spec=pltpu.PrefetchScalarGridSpec(
            num_scalar_prefetch=1,
            grid=(1,),
            in_specs=partner_specs(rows, wide, 0)
            + [
                pl.BlockSpec((rows, wide), lambda i, t: (0, 0)),
                pl.BlockSpec((out_rows, rows), lambda i, t: (0, t[0])),
                pl.BlockSpec((out_rows, rows), lambda i, t: (0, 1 - t[0])),
            ],
            out_specs=[
                pl.BlockSpec((rows, wide), lambda i, t: (0, 0)),
                pl.BlockSpec((rows, HD), lambda i, t: (0, 0)),
                pl.BlockSpec((out_rows, wide), lambda i, t: (0, 0)),
            ],
        ),
        out_shape=[
            jax.ShapeDtypeStruct((rows, wide), F32),
            jax.ShapeDtypeStruct((rows, HD), F32),
            jax.ShapeDtypeStruct((out_rows, wide), BF16),
        ],
        cost_estimate=cost(2 * 2 * 8 * rows * 2 * rows * HD, 3 << 20, 8 * rows * 2 * rows),
        name="attend_partner_a",
    )(place, query_a, partner_kv, partner_kv, key_rows, value_rows, att_own, picks, picks)


def partner_b_kernel(place, q_ref, kd, vd, ko, vo, sqo_ref, sqa_ref, att_ref, sum_ref, sq_ref):
    sq_ref[...] = sqa_ref[...]

    def put(head, value):
        att_ref[:, head * HD : (head + 1) * HD] = value
        sq_ref[...] += value * value

    attend_heads(q_ref, kd, vd, ko, vo, place[0] == 0, put)
    ones = jnp.ones((8, HD), F32)

    def lanes(values):
        return lax.dot_general(
            ones,
            values,
            (((1,), (1,)), ((), ())),
            precision=lax.Precision.HIGHEST,
            preferred_element_type=F32,
        )

    sum_ref[0:8, :] = lanes(sq_ref[...])
    sum_ref[8:16, :] = lanes(sqo_ref[0] + sqo_ref[1])


def attend_partner_b(place, query_b, partner_kv, key_rows, value_rows, sq_own, sq_a):
    rows, wide = query_b.shape
    return pl.pallas_call(
        partner_b_kernel,
        grid_spec=pltpu.PrefetchScalarGridSpec(
            num_scalar_prefetch=1,
            grid=(1,),
            in_specs=partner_specs(rows, wide, 1)
            + [
                pl.BlockSpec((2, rows, HD), lambda i, t: (0, 0, 0)),
                pl.BlockSpec((rows, HD), lambda i, t: (0, 0)),
            ],
            out_specs=[
                pl.BlockSpec((rows, wide), lambda i, t: (0, 0)),
                pl.BlockSpec((16, rows), lambda i, t: (0, 0)),
            ],
            scratch_shapes=[pltpu.VMEM((rows, HD), F32)],
        ),
        out_shape=[
            jax.ShapeDtypeStruct((rows, wide), F32),
            jax.ShapeDtypeStruct((16, rows), F32),
        ],
        cost_estimate=cost(2 * 2 * 8 * rows * 2 * rows * HD, 2 << 20, 8 * rows * 2 * rows),
        name="attend_partner_b",
    )(place, query_b, partner_kv, partner_kv, key_rows, value_rows, sq_own, sq_a)


def norm_kernel(
    place, own_ref, pa_ref, pb_ref, mine_ref, theirs_ref, gain_ref, so_ref, sp_ref, h_ref, out_ref
):
    rows = own_ref.shape[0]
    wide = pa_ref.shape[1]
    ones = jnp.full((8, HD), 0.125, F32)

    def scale_of(first, second):
        total = lax.dot_general(
            first + second,
            ones,
            (((0,), (0,)), ((), ())),
            precision=lax.Precision.HIGHEST,
            preferred_element_type=F32,
        )
        return lax.rsqrt(total * (1.0 / D) + EPSILON)

    lane = lax.broadcasted_iota(jnp.int32, (rows, HD), 1)

    def coded(scale):
        high = scale.astype(BF16)
        rest = scale - high.astype(F32)
        low = rest.astype(BF16)
        last = (rest - low.astype(F32)).astype(BF16)
        picked = jnp.where(lane == 0, high.astype(F32), 0.0)
        picked = jnp.where(lane == 1, low.astype(F32), picked)
        picked = jnp.where(lane == 2, last.astype(F32), picked)
        return jnp.where(lane == 3, 1.0, picked).astype(BF16)

    own_scale = scale_of(mine_ref[8:16, :], theirs_ref[0:8, :])
    other_scale = scale_of(mine_ref[0:8, :], theirs_ref[8:16, :])
    own_at = pl.ds(pl.multiple_of(place[0] * rows, rows), rows)
    other_at = pl.ds(pl.multiple_of((1 - place[0]) * rows, rows), rows)
    gain = gain_ref[...]
    h_ref[own_at, :] = (own_ref[...] * own_scale[:, 0:1] * gain).astype(BF16)
    h_ref[other_at, 0:wide] = (pa_ref[...] * other_scale[:, 0:1] * gain[:, 0:wide]).astype(BF16)
    h_ref[other_at, wide:] = (pb_ref[...] * other_scale[:, 0:1] * gain[:, wide:]).astype(BF16)
    picks_own = so_ref[...]
    picks_other = sp_ref[...]
    picked = dot(picks_own, h_ref[own_at, wide:]) + dot(picks_other, h_ref[other_at, wide:])
    out_ref[:, 0:wide] = picked.astype(BF16)
    extra = dot(picks_own, coded(own_scale)) + dot(picks_other, coded(other_scale))
    out_ref[:, wide:] = extra.astype(BF16)


def normalize(place, att_own, att_a, att_b, mine, theirs, norm_gain, picks):
    rows, half = att_own.shape
    wide = half // 2
    out_rows = picks.shape[0]
    whole = lambda i, t: (0, 0)
    return pl.pallas_call(
        norm_kernel,
        grid_spec=pltpu.PrefetchScalarGridSpec(
            num_scalar_prefetch=1,
            grid=(1,),
            in_specs=[
                pl.BlockSpec((rows, half), whole),
                pl.BlockSpec((rows, wide), whole),
                pl.BlockSpec((rows, wide), whole),
                pl.BlockSpec((16, rows), whole),
                pl.BlockSpec((16, rows), whole),
                pl.BlockSpec((1, half), lambda i, t: (0, t[0])),
                pl.BlockSpec((out_rows, rows), lambda i, t: (0, t[0])),
                pl.BlockSpec((out_rows, rows), lambda i, t: (0, 1 - t[0])),
            ],
            out_specs=[
                pl.BlockSpec((2 * rows, half), whole),
                pl.BlockSpec((out_rows, wide + EXTRA), whole),
            ],
        ),
        out_shape=[
            jax.ShapeDtypeStruct((2 * rows, half), BF16),
            jax.ShapeDtypeStruct((out_rows, wide + EXTRA), BF16),
        ],
        cost_estimate=cost(2 * out_rows * 2 * rows * wide, 8 << 20),
        name="normalize",
    )(place, att_own, att_a, att_b, mine, theirs, norm_gain, picks, picks)


def picks_kernel(col_ref, row_ref, key_ref, out_ref):
    tokens = row_ref.shape[1]
    label = row_ref[...]
    before = lax.broadcasted_iota(jnp.int32, (tokens, tokens), 0)
    at = lax.broadcasted_iota(jnp.int32, (tokens, tokens), 1)
    same = jnp.logical_and(col_ref[...] == label, before < at)
    rank = jnp.sum(jnp.where(same, 1, 0), axis=0, keepdims=True)
    token_key = jnp.where(jnp.logical_and(label < C, rank < 16), label * 16 + rank, -1)
    out_ref[...] = jnp.where(key_ref[...] == token_key, 1.0, 0.0).astype(BF16)


def class_picks(labels, classes):
    tokens = labels.shape[0]
    slots = jnp.arange(SLOT, dtype=jnp.int32)
    keys = (classes[:, :, None] * 16 + slots[None, None, :]).reshape(-1, 1)
    return pl.pallas_call(
        picks_kernel,
        in_specs=[VMEM_SPEC] * 3,
        out_specs=VMEM_SPEC,
        out_shape=jax.ShapeDtypeStruct((keys.shape[0], tokens), BF16),
        cost_estimate=cost(4 * tokens * tokens, 1 << 20),
        name="class_picks",
    )(labels.reshape(tokens, 1), labels.reshape(1, tokens), keys)


def gram_own_kernel(place, *refs):
    a_refs = refs[0:BLOCKS]
    b_refs = refs[BLOCKS : 2 * BLOCKS]
    gain_ref, out_ref, turned_ref, extra_ref, rows_ref = refs[2 * BLOCKS :]
    span = 2 * ROWS
    wide = a_refs[0].shape[1]
    step = out_ref.shape[0]

    @pl.when(pl.program_id(0) == 0)
    def _():
        for block in range(BLOCKS):
            at = slice(block * span, (block + 1) * span)
            extra = b_refs[block][:, wide:].astype(F32)
            extra_ref[at, :] = extra
            scale = extra[:, 0:1] + extra[:, 1:2] + extra[:, 2:3]
            scaled = a_refs[block][...].astype(F32) * scale * gain_ref[:, 0:wide]
            rows_ref[at, 0:wide] = scaled.astype(BF16)
            rows_ref[at, wide:] = b_refs[block][:, 0:wide]
        turned_ref[...] = jnp.transpose(rows_ref[...])

    count = jnp.sum(extra_ref[:, 3:4])
    left = turned_ref[pl.ds(pl.multiple_of(pl.program_id(0) * step, step), step), :]
    out_ref[...] = (dot(left, rows_ref[...]) * (1.0 / count)).astype(BF16)


def gram_own(place, pieces_a, pieces_b, norm_gain):
    wide = pieces_a[0].shape[1]
    half = 2 * wide
    total = BLOCKS * 2 * ROWS
    step = 512
    whole = lambda i, t: (0, 0)
    return pl.pallas_call(
        gram_own_kernel,
        grid_spec=pltpu.PrefetchScalarGridSpec(
            num_scalar_prefetch=1,
            grid=(half // step,),
            in_specs=[pl.BlockSpec((2 * ROWS, wide), whole)] * BLOCKS
            + [pl.BlockSpec((2 * ROWS, wide + EXTRA), whole)] * BLOCKS
            + [pl.BlockSpec((1, half), lambda i, t: (0, t[0]))],
            out_specs=[
                pl.BlockSpec((step, half), lambda i, t: (i, t[0])),
                pl.BlockSpec((half, total), whole),
                pl.BlockSpec((total, EXTRA), whole),
            ],
            scratch_shapes=[pltpu.VMEM((total, half), BF16)],
        ),
        out_shape=[
            jax.ShapeDtypeStruct((half, 2 * half), BF16),
            jax.ShapeDtypeStruct((half, total), BF16),
            jax.ShapeDtypeStruct((total, EXTRA), F32),
        ],
        cost_estimate=cost(2 * half * half * total, 14 << 20),
        name="gram_own",
    )(place, *pieces_a, *pieces_b, norm_gain)


def gram_other_kernel(place, *refs):
    a_refs = refs[0:BLOCKS]
    b_refs = refs[BLOCKS : 2 * BLOCKS]
    gain_ref, turned_ref, extra_ref, _, out_ref, rows_ref = refs[2 * BLOCKS :]
    span = 2 * ROWS
    wide = a_refs[0].shape[1]

    @pl.when(pl.program_id(0) == 0)
    def _():
        for block in range(BLOCKS):
            at = slice(block * span, (block + 1) * span)
            extra = extra_ref[at, :]
            scale = extra[:, 0:1] + extra[:, 1:2] + extra[:, 2:3]
            scaled = a_refs[block][...].astype(F32) * scale * gain_ref[:, 0:wide]
            rows_ref[at, 0:wide] = scaled.astype(BF16)
            rows_ref[at, wide:] = b_refs[block][...]

    count = jnp.sum(extra_ref[:, 3:4])
    out_ref[...] = (dot(turned_ref[...], rows_ref[...]) * (1.0 / count)).astype(BF16)


def gram_other(place, pieces_a, pieces_b, norm_gain, turned, extra, partial):
    wide = pieces_a[0].shape[1]
    half = 2 * wide
    total = BLOCKS * 2 * ROWS
    step = 512
    whole = lambda i, t: (0, 0)
    return pl.pallas_call(
        gram_other_kernel,
        grid_spec=pltpu.PrefetchScalarGridSpec(
            num_scalar_prefetch=1,
            grid=(half // step,),
            in_specs=[pl.BlockSpec((2 * ROWS, wide), whole)] * (2 * BLOCKS)
            + [
                pl.BlockSpec((1, half), lambda i, t: (0, 1 - t[0])),
                pl.BlockSpec((step, total), lambda i, t: (i, 0)),
                pl.BlockSpec((total, EXTRA), whole),
                pl.BlockSpec(memory_space=pl.ANY),
            ],
            out_specs=pl.BlockSpec((step, half), lambda i, t: (i, 1 - t[0])),
            scratch_shapes=[pltpu.VMEM((total, half), BF16)],
        ),
        out_shape=jax.ShapeDtypeStruct((half, 2 * half), BF16),
        input_output_aliases={2 * BLOCKS + 4: 0},
        cost_estimate=cost(2 * half * half * total, 14 << 20),
        name="gram_other",
    )(place, *pieces_a, *pieces_b, norm_gain, turned, extra, partial)


def paired_local(queries, key_rows, value_rows, norm_gain, labels, pair_list, owner_map):
    group_count = lax.axis_size("dp")
    my_tensor = lax.axis_index("tensor")
    my_group = lax.axis_index("dp")
    place = jnp.full((1,), my_tensor, jnp.int32)
    wide = D // KVH
    swap = [(0, 1), (1, 0)]

    def across(value):
        return lax.ppermute(value, "tensor", swap)

    def hop(value, offset):
        return lax.ppermute(value, "dp", [(i, i ^ offset) for i in range(group_count)])

    def theirs(rows, start, width):
        return lax.dynamic_slice_in_dim(rows, (1 - my_tensor) * start, width, 1)

    part = 2 * HD
    sent_kv = jnp.concatenate([theirs(key_rows, part, part), theirs(value_rows, part, part)], 1)
    partner_kv = across(sent_kv)
    other_half = (1 - my_tensor) * 2 * wide
    query_a = across(lax.dynamic_slice_in_dim(queries, other_half, wide, 1))
    query_b = across(lax.dynamic_slice_in_dim(queries, other_half + wide, wide, 1))

    order = jnp.concatenate([jnp.arange(0, 16, 2), jnp.arange(1, 16, 2)]).astype(jnp.int32)
    classes = pair_list[owner_map[my_group ^ order]]
    picks = class_picks(labels, classes)
    gain = norm_gain.reshape(1, D)

    def spread(rows):
        width = rows.shape[1]
        stay, leave = rows[: BLOCKS * ROWS], rows[BLOCKS * ROWS :]
        came = hop(leave, 1)
        joined = jnp.concatenate(
            [stay.reshape(BLOCKS, ROWS, width), came.reshape(BLOCKS, ROWS, width)], 1
        )
        return [joined[0]] + [hop(joined[m], 2 * m) for m in range(1, BLOCKS)]

    att_own, sq_own = attend_own(place, queries, key_rows, value_rows, partner_kv)
    att_a, sq_a, rows_a = attend_partner_a(
        place, query_a, partner_kv, key_rows, value_rows, att_own, picks
    )
    own_a = spread(rows_a)
    other_a = [across(piece) for piece in own_a]
    att_b, mine = attend_partner_b(place, query_b, partner_kv, key_rows, value_rows, sq_own, sq_a)
    harvest, rows_b = normalize(place, att_own, att_a, att_b, mine, across(mine), gain, picks)
    own_b = spread(rows_b)
    other_b = [across(piece[:, :wide]) for piece in own_b]
    partial, turned, extra = gram_own(place, own_a, own_b, gain)
    gram = gram_other(place, other_a, other_b, gain, turned, extra, partial)
    return gram[None], harvest


def solution(mesh):
    paired = mesh.shape["tensor"] == 2 and mesh.shape["dp"] == P_SIZE
    return jax.shard_map(
        paired_local if paired else general_local,
        mesh=mesh,
        in_specs=(
            P(("dp", "tensor"), None),
            P(("dp", "tensor"), None),
            P(("dp", "tensor"), None),
            P(),
            P("dp"),
            P(),
            P(),
        ),
        out_specs=(P("dp", "tensor", None), P("dp", "tensor")),
        check_vma=False,
    )
```

```python
import math

import jax
import jax.numpy as jnp
from jax import lax
from jax.experimental import pallas as pl
from jax.experimental.pallas import tpu as pltpu
from jax.sharding import PartitionSpec as P

H = 32
KVH = 4
HD = 128
D = 4096
C = 12
P_SIZE = 16
SLOT = 12


NEGATIVE = -1e30
EPSILON = 1e-06

BF16 = jnp.bfloat16
F32 = jnp.float32


def from_root(shard, axis, root):
    mine = lax.axis_index(axis) == root
    return lax.psum(jnp.where(mine, shard, jnp.zeros_like(shard)), axis)


def folded_keys(query_heads, key_heads, value_heads, offset, block_rows):
    local_rows, head_count, head_width = query_heads.shape
    kv_count = key_heads.shape[1]
    group_size = head_count // kv_count
    score_scale = 1.0 / math.sqrt(head_width)
    grouped = query_heads.reshape(local_rows, kv_count, group_size, head_width)
    positions = offset + jnp.arange(local_rows)
    initial = (
        jnp.full((kv_count, group_size, local_rows), NEGATIVE, jnp.float32),
        jnp.zeros((kv_count, group_size, local_rows), jnp.float32),
        jnp.zeros((kv_count, group_size, local_rows, head_width), jnp.float32),
    )
    pieces = (
        lax.all_gather(key_heads, "tensor", axis=0, tiled=True),
        lax.all_gather(value_heads, "tensor", axis=0, tiled=True),
    )
    piece_start = jnp.int32(0)

    def compute(state_in):
        row_max, row_total, accumulated = state_in
        key_piece, value_piece = pieces
        piece_rows = key_piece.shape[0]
        for sub_start in range(0, piece_rows, block_rows):
            key_block = key_piece[sub_start : sub_start + block_rows]
            value_block = value_piece[sub_start : sub_start + block_rows]
            span_rows = key_block.shape[0]
            scores = (
                jnp.einsum("skgd,nkd->kgsn", grouped, key_block, preferred_element_type=jnp.float32)
                * score_scale
            )
            key_places = piece_start + sub_start + jnp.arange(span_rows)
            allowed = key_places[None, :] <= positions[:, None]
            scores = jnp.where(allowed, scores, NEGATIVE)
            new_max = jnp.maximum(row_max, jnp.max(scores, axis=-1))
            expo_vals = jnp.where(allowed, jnp.exp(scores - new_max[..., None]), 0.0)
            factor = jnp.exp(row_max - new_max)
            row_total = row_total * factor + jnp.sum(expo_vals, axis=-1)
            accumulated = accumulated * factor[..., None] + jnp.einsum(
                "kgsn,nkd->kgsd",
                expo_vals.astype(jnp.bfloat16),
                value_block,
                preferred_element_type=jnp.float32,
            )
            row_max = new_max
        return (row_max, row_total, accumulated)

    row_max, row_total, accumulated = lax.cond(
        piece_start <= offset + local_rows - 1, compute, lambda state_in: state_in, initial
    )
    attended = accumulated / row_total[..., None]
    return jnp.transpose(attended, (2, 0, 1, 3)).reshape(local_rows, head_count * head_width)


def class_rows(harvest, labels, class_count, slot_count):
    seq_len = labels.shape[0]
    onehot = (labels[:, None] == jnp.arange(class_count, dtype=jnp.int32)[None, :]).astype(
        jnp.int32
    )
    ranks = jnp.cumsum(onehot, axis=0) - onehot
    picked = onehot[None, :, :] * (
        ranks[None, :, :] == jnp.arange(slot_count, dtype=jnp.int32)[:, None, None]
    ).astype(jnp.int32)
    positions = jnp.sum(picked * jnp.arange(seq_len, dtype=jnp.int32)[None, :, None], axis=1)
    present = jnp.sum(picked, axis=1)
    gathered = harvest[jnp.transpose(positions)]
    return gathered * jnp.transpose(present)[:, :, None].astype(harvest.dtype)


def general_local(queries, key_rows, value_rows, norm_gain, labels, pair_list, owner_map):
    tensor_count = lax.axis_size("tensor")
    group_count = lax.axis_size("dp")
    local_rows = queries.shape[0]
    seq_len = local_rows * tensor_count
    block_rows = min(seq_len, 512)
    part_width = D // tensor_count
    my_tensor = lax.axis_index("tensor")
    my_group = lax.axis_index("dp")
    query_heads = queries.reshape(local_rows, H, HD)
    key_heads = key_rows.reshape(local_rows, KVH, HD)
    value_heads = value_rows.reshape(local_rows, KVH, HD)
    attended = folded_keys(query_heads, key_heads, value_heads, my_tensor * local_rows, block_rows)
    squares = jnp.sum(attended * attended, axis=1)
    whole_rows = (attended * lax.rsqrt(squares / D + EPSILON)[:, None] * norm_gain[None, :]).astype(
        jnp.bfloat16
    )
    harvest = lax.all_to_all(whole_rows, "tensor", split_axis=1, concat_axis=0, tiled=True)
    class_ids = jnp.arange(C, dtype=jnp.int32)
    local_counts = jnp.sum((labels[:, None] == class_ids[None, :]).astype(jnp.float32), axis=0)
    counts = lax.psum(local_counts, "dp")
    per_class = class_rows(harvest, labels, C, SLOT)
    blocks_per_pair = group_count // P_SIZE
    dest_classes = pair_list[owner_map // blocks_per_pair]
    outgoing = per_class[dest_classes]
    incoming = lax.all_to_all(outgoing, "dp", split_axis=0, concat_axis=0, tiled=True)
    stacked = incoming.reshape(-1, part_width)
    my_block = owner_map[my_group]
    my_classes = pair_list[my_block // blocks_per_pair]
    my_share = my_block % blocks_per_pair
    pair_count = counts[my_classes[0]] + counts[my_classes[1]]
    slice_count = P_SIZE * tensor_count // group_count
    received = []
    for slot_index in range(slice_count):
        received.append(from_root(stacked, "tensor", my_share * slice_count + slot_index))
    chosen = jnp.concatenate(received, axis=1)
    tile = lax.dot_general(
        stacked, chosen, (((0,), (0,)), ((), ())), preferred_element_type=jnp.float32
    )
    return ((tile / pair_count).astype(jnp.bfloat16)[None], harvest)


ROWS = 2 * SLOT
EARLY = (8, 12, 9, 13)
LATE = (0, 2, 4, 6, 10, 14)
EARLY_ROWS = len(EARLY) * ROWS
LATE_ROWS = len(LATE) * ROWS
PIECES = len(EARLY) // 2 + len(LATE)
SPAN = 2 * ROWS
ABSENT = 2.0**100
WIDE_A = 12 * HD
VMEM_SPEC = pl.BlockSpec(memory_space=pltpu.VMEM)


def nt(left, right):
    return lax.dot_general(left, right, (((1,), (1,)), ((), ())), preferred_element_type=F32)


def dot(left, right):
    return lax.dot_general(left, right, (((1,), (0,)), ((), ())), preferred_element_type=F32)


def attend_heads(q_ref, first, kd, vd, ko, vo, use_off, put):
    rows = q_ref.shape[0]
    heads = q_ref.shape[1] // HD
    factor = math.log2(math.e) / math.sqrt(HD)

    def run(with_off):
        row = lax.broadcasted_iota(jnp.int32, (rows, rows), 0)
        col = lax.broadcasted_iota(jnp.int32, (rows, rows), 1)
        allowed = col <= row
        for head in range(heads):
            query = q_ref[:, head * HD : (head + 1) * HD]
            key_head = (first + head) // (H // KVH)
            at = slice(key_head * HD, (key_head + 1) * HD)
            diag = jnp.where(allowed, nt(query, kd[:, at]), NEGATIVE)
            peak = jnp.max(diag, axis=-1, keepdims=True)
            if with_off:
                off = nt(query, ko[:, at])
                peak = jnp.maximum(peak, jnp.max(off, axis=-1, keepdims=True))
            diag_w = jnp.exp2((diag - peak) * factor)
            total = jnp.sum(diag_w, axis=-1, keepdims=True)
            mixed = dot(diag_w.astype(BF16), vd[:, at])
            if with_off:
                off_w = jnp.exp2((off - peak) * factor)
                total = total + jnp.sum(off_w, axis=-1, keepdims=True)
                mixed = mixed + dot(off_w.astype(BF16), vo[:, at])
            put(head, mixed * (1.0 / total))

    @pl.when(use_off)
    def _():
        run(True)

    @pl.when(jnp.logical_not(use_off))
    def _():
        run(False)


def own_kernel(place, q_ref, k_ref, v_ref, kp_ref, vp_ref, att_ref, sq_ref):
    sq_ref[...] = jnp.zeros_like(sq_ref)

    def put(head, value):
        att_ref[:, head * HD : (head + 1) * HD] = value
        sq_ref[0] += value * value

    attend_heads(q_ref, 0, k_ref, v_ref, kp_ref, vp_ref, place[0] == 1, put)


def attend_own(place, queries, key_rows, value_rows, partner_kv):
    rows = queries.shape[0]
    wide = D // KVH
    return pl.pallas_call(
        own_kernel,
        grid_spec=pltpu.PrefetchScalarGridSpec(
            num_scalar_prefetch=1,
            grid=(2,),
            in_specs=[
                pl.BlockSpec((rows, wide), lambda i, t: (0, 2 * t[0] + i)),
                pl.BlockSpec((rows, HD), lambda i, t: (0, 2 * t[0] + i)),
                pl.BlockSpec((rows, HD), lambda i, t: (0, 2 * t[0] + i)),
                pl.BlockSpec((rows, HD), lambda i, t: (0, i)),
                pl.BlockSpec((rows, HD), lambda i, t: (0, 2 + i)),
            ],
            out_specs=[
                pl.BlockSpec((rows, wide), lambda i, t: (0, i)),
                pl.BlockSpec((1, rows, HD), lambda i, t: (i, 0, 0)),
            ],
        ),
        out_shape=[
            jax.ShapeDtypeStruct((rows, 2 * wide), F32),
            jax.ShapeDtypeStruct((2, rows, HD), F32),
        ],
        name="attend_own",
    )(place, queries, key_rows, value_rows, partner_kv, partner_kv)


def absent_of(first, second):
    present = jnp.sum(first.astype(F32) + second.astype(F32), axis=-1, keepdims=True)
    return (1.0 - present) * ABSENT


def partner_a_kernel(
    place, q_ref, kd, vd, ko, vo, own_ref, so_ref, sp_ref, att_ref, sq_ref, out_ref
):
    wide = q_ref.shape[1]
    sq_ref[...] = jnp.zeros_like(sq_ref)

    def put(head, value):
        att_ref[:, head * HD : (head + 1) * HD] = value
        sq_ref[...] += value * value

    attend_heads(q_ref, 0, kd, vd, ko, vo, place[0] == 0, put)
    picked = dot(so_ref[...], own_ref[...].astype(BF16))
    out_ref[:, wide:] = picked[:, wide:].astype(BF16)
    picked = picked[:, 0:wide] + dot(sp_ref[...], att_ref[...].astype(BF16))
    out_ref[:, 0:wide] = picked.astype(BF16)


def partner_specs(rows, wide):
    return [
        pl.BlockSpec((rows, wide), lambda i, t: (0, 0)),
        pl.BlockSpec((rows, 2 * HD), lambda i, t: (0, 0)),
        pl.BlockSpec((rows, 2 * HD), lambda i, t: (0, 1)),
        pl.BlockSpec((rows, 2 * HD), lambda i, t: (0, t[0])),
        pl.BlockSpec((rows, 2 * HD), lambda i, t: (0, t[0])),
    ]


def attend_partner_a(place, query_a, partner_kv, key_rows, value_rows, att_own, picks):
    rows, wide = query_a.shape
    half = att_own.shape[1]
    return pl.pallas_call(
        partner_a_kernel,
        grid_spec=pltpu.PrefetchScalarGridSpec(
            num_scalar_prefetch=1,
            grid=(1,),
            in_specs=partner_specs(rows, wide)
            + [
                pl.BlockSpec((rows, half), lambda i, t: (0, 0)),
                pl.BlockSpec((EARLY_ROWS, rows), lambda i, t: (0, t[0])),
                pl.BlockSpec((EARLY_ROWS, rows), lambda i, t: (0, 1 - t[0])),
            ],
            out_specs=[
                pl.BlockSpec((rows, wide), lambda i, t: (0, 0)),
                pl.BlockSpec((rows, HD), lambda i, t: (0, 0)),
                pl.BlockSpec((EARLY_ROWS, half), lambda i, t: (0, 0)),
            ],
        ),
        out_shape=[
            jax.ShapeDtypeStruct((rows, wide), F32),
            jax.ShapeDtypeStruct((rows, HD), F32),
            jax.ShapeDtypeStruct((EARLY_ROWS, half), BF16),
        ],
        name="attend_partner_a",
    )(place, query_a, partner_kv, partner_kv, key_rows, value_rows, att_own, picks, picks)


def partner_b_kernel(place, q_ref, kd, vd, ko, vo, sqo_ref, sqa_ref, so_ref, sp_ref, early_ref, *refs):
    att_ref, sum_ref = refs[0:2]
    out_refs, sq_ref = refs[2:-1], refs[-1]
    wide = early_ref.shape[1] - q_ref.shape[1]
    sq_ref[...] = sqa_ref[...]

    def put(head, value):
        att_ref[:, head * HD : (head + 1) * HD] = value
        sq_ref[...] += value * value

    first = H // 2 - q_ref.shape[1] // HD
    attend_heads(q_ref, first, kd, vd, ko, vo, place[0] == 0, put)
    absent = absent_of(so_ref[...], sp_ref[...])
    picked = dot(sp_ref[...], att_ref[...].astype(BF16)) + early_ref[:, wide:].astype(F32)
    picked = (picked + absent).astype(BF16)
    early = (early_ref[:, 0:wide].astype(F32) + absent).astype(BF16)
    for index, out_ref in enumerate(out_refs):
        at = slice(index * ROWS, (index + 1) * ROWS)
        out_ref[:, 0:wide] = early[at]
        out_ref[:, wide:] = picked[at]
    ones = jnp.ones((8, HD), F32)

    def lanes(values):
        return lax.dot_general(
            ones,
            values,
            (((1,), (1,)), ((), ())),
            precision=lax.Precision.HIGHEST,
            preferred_element_type=F32,
        )

    sum_ref[0:8, :] = lanes(sq_ref[...])
    sum_ref[8:16, :] = lanes(sqo_ref[0] + sqo_ref[1])


def attend_partner_b(
    place, query_b, partner_kv, key_rows, value_rows, sq_own, sq_a, picks, early_a
):
    rows, wide = query_b.shape
    half = early_a.shape[1]
    whole = lambda i, t: (0, 0)
    return pl.pallas_call(
        partner_b_kernel,
        grid_spec=pltpu.PrefetchScalarGridSpec(
            num_scalar_prefetch=1,
            grid=(1,),
            in_specs=partner_specs(rows, wide)
            + [
                pl.BlockSpec((2, rows, HD), lambda i, t: (0, 0, 0)),
                pl.BlockSpec((rows, HD), whole),
                pl.BlockSpec((EARLY_ROWS, rows), lambda i, t: (0, t[0])),
                pl.BlockSpec((EARLY_ROWS, rows), lambda i, t: (0, 1 - t[0])),
                pl.BlockSpec((EARLY_ROWS, half), whole),
            ],
            out_specs=[
                pl.BlockSpec((rows, wide), whole),
                pl.BlockSpec((16, rows), whole),
            ]
            + [pl.BlockSpec((ROWS, half), whole)] * len(EARLY),
            scratch_shapes=[pltpu.VMEM((rows, HD), F32)],
        ),
        out_shape=[
            jax.ShapeDtypeStruct((rows, wide), F32),
            jax.ShapeDtypeStruct((16, rows), F32),
        ]
        + [jax.ShapeDtypeStruct((ROWS, half), BF16)] * len(EARLY),
        name="attend_partner_b",
    )(
        place, query_b, partner_kv, partner_kv, key_rows, value_rows,
        sq_own, sq_a, picks, picks, early_a,
    )


def norm_kernel(
    place, own_ref, pa_ref, pb_ref, mine_ref, theirs_ref, gain_ref, so_ref, sp_ref,
    h_ref, stay_ref, leave_ref,
):
    rows = own_ref.shape[0]
    wide = pa_ref.shape[1]
    ones = jnp.full((8, HD), 0.125, F32)

    def scale_of(first, second):
        total = lax.dot_general(
            first + second,
            ones,
            (((0,), (0,)), ((), ())),
            precision=lax.Precision.HIGHEST,
            preferred_element_type=F32,
        )
        return lax.rsqrt(total * (1.0 / D) + EPSILON)[:, 0:1]

    own_scale = scale_of(mine_ref[8:16, :], theirs_ref[0:8, :])
    other_scale = scale_of(mine_ref[0:8, :], theirs_ref[8:16, :])
    own_at = pl.ds(pl.multiple_of(place[0] * rows, rows), rows)
    other_at = pl.ds(pl.multiple_of((1 - place[0]) * rows, rows), rows)
    gain = gain_ref[...]
    h_ref[own_at, :] = (own_ref[...] * own_scale * gain).astype(BF16)
    h_ref[other_at, 0:wide] = (pa_ref[...] * other_scale * gain[:, 0:wide]).astype(BF16)
    h_ref[other_at, wide:] = (pb_ref[...] * other_scale * gain[:, wide:]).astype(BF16)
    start = EARLY_ROWS
    for out_ref in (stay_ref, leave_ref):
        first = so_ref[start : start + LATE_ROWS, :]
        second = sp_ref[start : start + LATE_ROWS, :]
        picked = dot(first, h_ref[own_at, :]) + dot(second, h_ref[other_at, :])
        out_ref[...] = (picked + absent_of(first, second)).astype(BF16)
        start += LATE_ROWS


def normalize(place, att_own, att_a, att_b, mine, theirs, norm_gain, picks):
    rows, half = att_own.shape
    wide, last = att_a.shape[1], att_b.shape[1]
    all_rows = picks.shape[0]
    whole = lambda i, t: (0, 0)
    return pl.pallas_call(
        norm_kernel,
        grid_spec=pltpu.PrefetchScalarGridSpec(
            num_scalar_prefetch=1,
            grid=(1,),
            in_specs=[
                pl.BlockSpec((rows, half), whole),
                pl.BlockSpec((rows, wide), whole),
                pl.BlockSpec((rows, last), whole),
                pl.BlockSpec((16, rows), whole),
                pl.BlockSpec((16, rows), whole),
                pl.BlockSpec((1, half), lambda i, t: (0, t[0])),
                pl.BlockSpec((all_rows, rows), lambda i, t: (0, t[0])),
                pl.BlockSpec((all_rows, rows), lambda i, t: (0, 1 - t[0])),
            ],
            out_specs=[
                pl.BlockSpec((2 * rows, half), whole),
                pl.BlockSpec((LATE_ROWS, half), whole),
                pl.BlockSpec((LATE_ROWS, half), whole),
            ],
        ),
        out_shape=[
            jax.ShapeDtypeStruct((2 * rows, half), BF16),
            jax.ShapeDtypeStruct((LATE_ROWS, half), BF16),
            jax.ShapeDtypeStruct((LATE_ROWS, half), BF16),
        ],
        name="normalize",
    )(place, att_own, att_a, att_b, mine, theirs, norm_gain, picks, picks)


def picks_kernel(col_ref, row_ref, key_ref, out_ref):
    tokens = row_ref.shape[1]
    label = row_ref[...]
    before = lax.broadcasted_iota(jnp.int32, (tokens, tokens), 0)
    at = lax.broadcasted_iota(jnp.int32, (tokens, tokens), 1)
    same = jnp.logical_and(col_ref[...] == label, before < at)
    rank = jnp.sum(jnp.where(same, 1, 0), axis=0, keepdims=True)
    token_key = jnp.where(jnp.logical_and(label < C, rank < 16), label * 16 + rank, -1)
    out_ref[...] = jnp.where(key_ref[...] == token_key, 1.0, 0.0).astype(BF16)


def class_picks(labels, classes):
    tokens = labels.shape[0]
    slots = jnp.arange(SLOT, dtype=jnp.int32)
    keys = (classes[:, :, None] * 16 + slots[None, None, :]).reshape(-1, 1)
    return pl.pallas_call(
        picks_kernel,
        in_specs=[VMEM_SPEC] * 3,
        out_specs=VMEM_SPEC,
        out_shape=jax.ShapeDtypeStruct((keys.shape[0], tokens), BF16),
        name="class_picks",
    )(labels.reshape(tokens, 1), labels.reshape(1, tokens), keys)


def gram_own_kernel(place, *refs):
    own_refs, across_refs = refs[0:PIECES], refs[PIECES : PIECES + 2]
    gain_ref, out_ref, turned_ref, extra_ref, rows_ref = refs[PIECES + 2 :]
    step = out_ref.shape[0]

    @pl.when(pl.program_id(0) == 0)
    def _():
        lane = lax.broadcasted_iota(jnp.int32, (SPAN, HD), 1)
        for piece in range(PIECES):
            at = slice(piece * SPAN, (piece + 1) * SPAN)
            present = own_refs[piece][:, 0:1].astype(F32) < 0.5 * ABSENT
            rows = jnp.where(present, own_refs[piece][...].astype(F32), 0.0)
            if piece < 2:
                other = jnp.where(present, across_refs[piece][...].astype(F32), 0.0)
                squares = jnp.sum(rows * rows + other * other, axis=-1, keepdims=True)
                scale = lax.rsqrt(squares * (1.0 / D) + EPSILON)
                rows = rows * scale * gain_ref[...]
            else:
                scale = jnp.ones((SPAN, 1), F32)
            rows_ref[at, :] = rows.astype(BF16)
            flag = jnp.where(present, 1.0, 0.0)
            extra_ref[at, :] = jnp.where(lane == 0, scale, jnp.where(lane == 1, flag, 0.0))
        turned_ref[...] = jnp.transpose(rows_ref[...])

    count = jnp.sum(extra_ref[:, 1:2])
    left = turned_ref[pl.ds(pl.multiple_of(pl.program_id(0) * step, step), step), :]
    out_ref[...] = (dot(left, rows_ref[...]) * (1.0 / count)).astype(BF16)


def gram_own(place, pieces, across_pieces, norm_gain):
    half = pieces[0].shape[1]
    total = PIECES * SPAN
    step = 512
    whole = lambda i, t: (0, 0)
    return pl.pallas_call(
        gram_own_kernel,
        grid_spec=pltpu.PrefetchScalarGridSpec(
            num_scalar_prefetch=1,
            grid=(half // step,),
            in_specs=[pl.BlockSpec((SPAN, half), whole)] * (PIECES + 2)
            + [pl.BlockSpec((1, half), lambda i, t: (0, t[0]))],
            out_specs=[
                pl.BlockSpec((step, half), lambda i, t: (i, t[0])),
                pl.BlockSpec((half, total), whole),
                pl.BlockSpec((total, HD), whole),
            ],
            scratch_shapes=[pltpu.VMEM((total, half), BF16)],
        ),
        out_shape=[
            jax.ShapeDtypeStruct((half, 2 * half), BF16),
            jax.ShapeDtypeStruct((half, total), BF16),
            jax.ShapeDtypeStruct((total, HD), F32),
        ],
        name="gram_own",
    )(place, *pieces, *across_pieces, norm_gain)


def gram_other_kernel(place, *refs):
    other_refs = refs[0:PIECES]
    gain_ref, turned_ref, extra_ref, _, out_ref, rows_ref = refs[PIECES:]

    @pl.when(pl.program_id(0) == 0)
    def _():
        for piece in range(PIECES):
            at = slice(piece * SPAN, (piece + 1) * SPAN)
            rows = other_refs[piece][...].astype(F32)
            if piece < 2:
                rows = rows * extra_ref[at, 0:1] * gain_ref[...]
            rows_ref[at, :] = jnp.where(extra_ref[at, 1:2] > 0.5, rows, 0.0).astype(BF16)

    count = jnp.sum(extra_ref[:, 1:2])
    out_ref[...] = (dot(turned_ref[...], rows_ref[...]) * (1.0 / count)).astype(BF16)


def gram_other(place, pieces, norm_gain, turned, extra, partial):
    half = pieces[0].shape[1]
    total = PIECES * SPAN
    step = 512
    whole = lambda i, t: (0, 0)
    return pl.pallas_call(
        gram_other_kernel,
        grid_spec=pltpu.PrefetchScalarGridSpec(
            num_scalar_prefetch=1,
            grid=(half // step,),
            in_specs=[pl.BlockSpec((SPAN, half), whole)] * PIECES
            + [
                pl.BlockSpec((1, half), lambda i, t: (0, 1 - t[0])),
                pl.BlockSpec((step, total), lambda i, t: (i, 0)),
                pl.BlockSpec((total, HD), whole),
                pl.BlockSpec(memory_space=pl.ANY),
            ],
            out_specs=pl.BlockSpec((step, half), lambda i, t: (i, 1 - t[0])),
            scratch_shapes=[pltpu.VMEM((total, half), BF16)],
        ),
        out_shape=jax.ShapeDtypeStruct((half, 2 * half), BF16),
        input_output_aliases={PIECES + 4: 0},
        name="gram_other",
    )(place, *pieces, norm_gain, turned, extra, partial)


def after(value, *earlier):
    return lax.optimization_barrier((value, *earlier))[0]


def paired_local(queries, key_rows, value_rows, norm_gain, labels, pair_list, owner_map):
    group_count = lax.axis_size("dp")
    my_tensor = lax.axis_index("tensor")
    my_group = lax.axis_index("dp")
    place = jnp.full((1,), my_tensor, jnp.int32)
    swap = [(0, 1), (1, 0)]

    def across(value, name):
        with jax.named_scope(name):
            return lax.ppermute(value, "tensor", swap)

    def hop(value, offset, name):
        with jax.named_scope(name):
            return lax.ppermute(value, "dp", [(i, i ^ offset) for i in range(group_count)])

    def theirs(rows, start, width):
        return lax.dynamic_slice_in_dim(rows, (1 - my_tensor) * start, width, 1)

    part = 2 * HD
    sent_kv = jnp.concatenate([theirs(key_rows, part, part), theirs(value_rows, part, part)], 1)
    partner_kv = across(sent_kv, "x_kv")
    other_half = (1 - my_tensor) * (D // 2)
    last = D // 2 - WIDE_A
    sent_a = lax.dynamic_slice_in_dim(queries, other_half, WIDE_A, 1)
    sent_b = lax.dynamic_slice_in_dim(queries, other_half + WIDE_A, last, 1)
    query_a = across(sent_a, "x_qa")
    query_b = across(after(sent_b, partner_kv), "x_qb")

    order = jnp.asarray(EARLY + LATE + tuple(j + 1 for j in LATE), jnp.int32)
    classes = pair_list[owner_map[my_group ^ order]]
    picks = class_picks(labels, classes)
    gain = norm_gain.reshape(1, D)

    att_own, sq_own = attend_own(place, queries, key_rows, value_rows, partner_kv)
    att_a, sq_a, early_a = attend_partner_a(
        place, query_a, partner_kv, key_rows, value_rows, att_own, picks
    )
    att_b, mine, *early = attend_partner_b(
        place, query_b, partner_kv, key_rows, value_rows, sq_own, sq_a, picks, early_a
    )
    first = [hop(rows, j, f"far_e{j}") for rows, j in zip(early, EARLY)]
    sums = after(across(mine, "x_sums"), first[0])
    harvest, stay, leave = normalize(place, att_own, att_a, att_b, mine, sums, gain, picks)
    came = hop(after(leave, first[1]), 1, "core")
    shape = (len(LATE), ROWS, D // 2)
    joined = jnp.concatenate([stay.reshape(shape), came.reshape(shape)], 1)
    joined = {j: joined[index] for index, j in enumerate(LATE)}
    own, other = {0: joined[0]}, {}
    pairs = [jnp.concatenate(first[0:2]), jnp.concatenate(first[2:4])]

    def far(j, *earlier):
        own[j] = hop(after(joined[j], *earlier), j, f"far_{j}")

    x_e0 = across(pairs[0], "x_e0")
    other[0] = across(own[0], "x_0")
    far(10, first[0])
    far(2, first[1])
    x_e1 = across(after(pairs[1], x_e0), "x_e1")
    far(14, first[2], x_e0)
    other[2] = across(after(own[2], other[0]), "x_2")
    far(4, own[2], other[0])
    other[10] = across(after(own[10], x_e1), "x_10")
    far(6, own[10], x_e1)
    other[4] = across(after(own[4], other[2]), "x_4")
    other[6] = across(after(own[6], other[10]), "x_6")
    other[14] = across(after(own[14], other[4]), "x_14")
    partial, turned, extra = gram_own(
        place, [*pairs, *[own[j] for j in LATE]], [x_e0, x_e1], gain
    )
    gram = gram_other(
        place, [x_e0, x_e1, *[other[j] for j in LATE]], gain, turned, extra, partial
    )
    return gram[None], harvest


def solution(mesh):
    paired = mesh.shape["tensor"] == 2 and mesh.shape["dp"] == P_SIZE
    return jax.shard_map(
        paired_local if paired else general_local,
        mesh=mesh,
        in_specs=(
            P(("dp", "tensor"), None),
            P(("dp", "tensor"), None),
            P(("dp", "tensor"), None),
            P(),
            P("dp"),
            P(),
            P(),
        ),
        out_specs=(P("dp", "tensor", None), P("dp", "tensor")),
        check_vma=False,
    )
```

```python
import math

import jax
import jax.numpy as jnp
from jax import lax
from jax.experimental import pallas as pl
from jax.experimental.pallas import tpu as pltpu
from jax.sharding import PartitionSpec as P

H = 32
KVH = 4
HD = 128
D = 4096
C = 12
P_SIZE = 16
SLOT = 12


NEGATIVE = -1e30
EPSILON = 1e-06

BF16 = jnp.bfloat16
F32 = jnp.float32


def from_root(shard, axis, root):
    mine = lax.axis_index(axis) == root
    return lax.psum(jnp.where(mine, shard, jnp.zeros_like(shard)), axis)


def folded_keys(query_heads, key_heads, value_heads, offset, block_rows):
    local_rows, head_count, head_width = query_heads.shape
    kv_count = key_heads.shape[1]
    group_size = head_count // kv_count
    score_scale = 1.0 / math.sqrt(head_width)
    grouped = query_heads.reshape(local_rows, kv_count, group_size, head_width)
    positions = offset + jnp.arange(local_rows)
    initial = (
        jnp.full((kv_count, group_size, local_rows), NEGATIVE, jnp.float32),
        jnp.zeros((kv_count, group_size, local_rows), jnp.float32),
        jnp.zeros((kv_count, group_size, local_rows, head_width), jnp.float32),
    )
    pieces = (
        lax.all_gather(key_heads, "tensor", axis=0, tiled=True),
        lax.all_gather(value_heads, "tensor", axis=0, tiled=True),
    )
    piece_start = jnp.int32(0)

    def compute(state_in):
        row_max, row_total, accumulated = state_in
        key_piece, value_piece = pieces
        piece_rows = key_piece.shape[0]
        for sub_start in range(0, piece_rows, block_rows):
            key_block = key_piece[sub_start : sub_start + block_rows]
            value_block = value_piece[sub_start : sub_start + block_rows]
            span_rows = key_block.shape[0]
            scores = (
                jnp.einsum("skgd,nkd->kgsn", grouped, key_block, preferred_element_type=jnp.float32)
                * score_scale
            )
            key_places = piece_start + sub_start + jnp.arange(span_rows)
            allowed = key_places[None, :] <= positions[:, None]
            scores = jnp.where(allowed, scores, NEGATIVE)
            new_max = jnp.maximum(row_max, jnp.max(scores, axis=-1))
            expo_vals = jnp.where(allowed, jnp.exp(scores - new_max[..., None]), 0.0)
            factor = jnp.exp(row_max - new_max)
            row_total = row_total * factor + jnp.sum(expo_vals, axis=-1)
            accumulated = accumulated * factor[..., None] + jnp.einsum(
                "kgsn,nkd->kgsd",
                expo_vals.astype(jnp.bfloat16),
                value_block,
                preferred_element_type=jnp.float32,
            )
            row_max = new_max
        return (row_max, row_total, accumulated)

    row_max, row_total, accumulated = lax.cond(
        piece_start <= offset + local_rows - 1, compute, lambda state_in: state_in, initial
    )
    attended = accumulated / row_total[..., None]
    return jnp.transpose(attended, (2, 0, 1, 3)).reshape(local_rows, head_count * head_width)


def class_rows(harvest, labels, class_count, slot_count):
    seq_len = labels.shape[0]
    onehot = (labels[:, None] == jnp.arange(class_count, dtype=jnp.int32)[None, :]).astype(
        jnp.int32
    )
    ranks = jnp.cumsum(onehot, axis=0) - onehot
    picked = onehot[None, :, :] * (
        ranks[None, :, :] == jnp.arange(slot_count, dtype=jnp.int32)[:, None, None]
    ).astype(jnp.int32)
    positions = jnp.sum(picked * jnp.arange(seq_len, dtype=jnp.int32)[None, :, None], axis=1)
    present = jnp.sum(picked, axis=1)
    gathered = harvest[jnp.transpose(positions)]
    return gathered * jnp.transpose(present)[:, :, None].astype(harvest.dtype)


def general_local(queries, key_rows, value_rows, norm_gain, labels, pair_list, owner_map):
    tensor_count = lax.axis_size("tensor")
    group_count = lax.axis_size("dp")
    local_rows = queries.shape[0]
    seq_len = local_rows * tensor_count
    block_rows = min(seq_len, 512)
    part_width = D // tensor_count
    my_tensor = lax.axis_index("tensor")
    my_group = lax.axis_index("dp")
    query_heads = queries.reshape(local_rows, H, HD)
    key_heads = key_rows.reshape(local_rows, KVH, HD)
    value_heads = value_rows.reshape(local_rows, KVH, HD)
    attended = folded_keys(query_heads, key_heads, value_heads, my_tensor * local_rows, block_rows)
    squares = jnp.sum(attended * attended, axis=1)
    whole_rows = (attended * lax.rsqrt(squares / D + EPSILON)[:, None] * norm_gain[None, :]).astype(
        jnp.bfloat16
    )
    harvest = lax.all_to_all(whole_rows, "tensor", split_axis=1, concat_axis=0, tiled=True)
    class_ids = jnp.arange(C, dtype=jnp.int32)
    local_counts = jnp.sum((labels[:, None] == class_ids[None, :]).astype(jnp.float32), axis=0)
    counts = lax.psum(local_counts, "dp")
    per_class = class_rows(harvest, labels, C, SLOT)
    blocks_per_pair = group_count // P_SIZE
    dest_classes = pair_list[owner_map // blocks_per_pair]
    outgoing = per_class[dest_classes]
    incoming = lax.all_to_all(outgoing, "dp", split_axis=0, concat_axis=0, tiled=True)
    stacked = incoming.reshape(-1, part_width)
    my_block = owner_map[my_group]
    my_classes = pair_list[my_block // blocks_per_pair]
    my_share = my_block % blocks_per_pair
    pair_count = counts[my_classes[0]] + counts[my_classes[1]]
    slice_count = P_SIZE * tensor_count // group_count
    received = []
    for slot_index in range(slice_count):
        received.append(from_root(stacked, "tensor", my_share * slice_count + slot_index))
    chosen = jnp.concatenate(received, axis=1)
    tile = lax.dot_general(
        stacked, chosen, (((0,), (0,)), ((), ())), preferred_element_type=jnp.float32
    )
    return ((tile / pair_count).astype(jnp.bfloat16)[None], harvest)


ROWS = 2 * SLOT
EARLY = (0, 1, 2, 3, 8, 9, 12, 13)
LATE = (4, 6, 10, 14)
EARLY_ROWS = len(EARLY) * ROWS
LATE_ROWS = len(LATE) * ROWS
SPAN = 2 * ROWS
PAIRS = len(EARLY) // 2
PIECES = PAIRS + len(LATE)
ABSENT = 2.0**100
WIDE_A = 12 * HD
VMEM_SPEC = pl.BlockSpec(memory_space=pltpu.VMEM)


def nt(left, right):
    return lax.dot_general(left, right, (((1,), (1,)), ((), ())), preferred_element_type=F32)


def dot(left, right):
    return lax.dot_general(left, right, (((1,), (0,)), ((), ())), preferred_element_type=F32)


def attend_heads(q_ref, first, kd, vd, ko, vo, use_off, att_ref, put_squares):
    rows = q_ref.shape[0]
    heads = q_ref.shape[1] // HD
    factor = math.log2(math.e) / math.sqrt(HD)

    def place_of(head):
        key_head = (first + head) // (H // KVH)
        return slice(key_head * HD, (key_head + 1) * HD)

    def run(with_off):
        row = lax.broadcasted_iota(jnp.int32, (rows, rows), 0)
        col = lax.broadcasted_iota(jnp.int32, (rows, rows), 1)
        allowed = col <= row

        def scores_of(head):
            query = q_ref[:, head * HD : (head + 1) * HD]
            at = place_of(head)
            return nt(query, kd[:, at]), nt(query, ko[:, at]) if with_off else None

        following = scores_of(0)
        squares = jnp.zeros((rows, HD), F32)
        for head in range(heads):
            (diag, off), at = following, place_of(head)
            if head + 1 < heads:
                following = scores_of(head + 1)
            diag = jnp.where(allowed, diag, NEGATIVE)
            both = jnp.maximum(diag, off) if with_off else diag
            peak = jnp.max(both, axis=-1, keepdims=True)
            weights = jnp.exp2((diag - peak) * factor)
            mixed = dot(weights.astype(BF16), vd[:, at])
            if with_off:
                off_weights = jnp.exp2((off - peak) * factor)
                mixed = mixed + dot(off_weights.astype(BF16), vo[:, at])
                weights = weights + off_weights
            value = mixed * (1.0 / jnp.sum(weights, axis=-1, keepdims=True))
            att_ref[:, head * HD : (head + 1) * HD] = value
            squares = squares + value * value
        put_squares(squares)

    @pl.when(use_off)
    def _():
        run(True)

    @pl.when(jnp.logical_not(use_off))
    def _():
        run(False)


def own_kernel(place, q_ref, k_ref, v_ref, kp_ref, vp_ref, att_ref, sq_ref):
    def put(squares):
        sq_ref[0] = squares

    attend_heads(q_ref, 0, k_ref, v_ref, kp_ref, vp_ref, place[0] == 1, att_ref, put)


def attend_own(place, queries, key_rows, value_rows, partner_kv):
    rows = queries.shape[0]
    wide = D // KVH
    return pl.pallas_call(
        own_kernel,
        grid_spec=pltpu.PrefetchScalarGridSpec(
            num_scalar_prefetch=1,
            grid=(2,),
            in_specs=[
                pl.BlockSpec((rows, wide), lambda i, t: (0, 2 * t[0] + i)),
                pl.BlockSpec((rows, HD), lambda i, t: (0, 2 * t[0] + i)),
                pl.BlockSpec((rows, HD), lambda i, t: (0, 2 * t[0] + i)),
                pl.BlockSpec((rows, HD), lambda i, t: (0, i)),
                pl.BlockSpec((rows, HD), lambda i, t: (0, 2 + i)),
            ],
            out_specs=[
                pl.BlockSpec((rows, wide), lambda i, t: (0, i)),
                pl.BlockSpec((1, rows, HD), lambda i, t: (i, 0, 0)),
            ],
        ),
        out_shape=[
            jax.ShapeDtypeStruct((rows, 2 * wide), F32),
            jax.ShapeDtypeStruct((2, rows, HD), F32),
        ],
        name="attend_own",
    )(place, queries, key_rows, value_rows, partner_kv, partner_kv)


def absent_of(first, second):
    present = jnp.sum(first.astype(F32) + second.astype(F32), axis=-1, keepdims=True)
    return (1.0 - present) * ABSENT


def partner_a_kernel(
    place, q_ref, kd, vd, ko, vo, own_ref, so_ref, sp_ref, att_ref, sq_ref, out_ref
):
    wide = q_ref.shape[1]

    def put(squares):
        sq_ref[...] = squares

    attend_heads(q_ref, 0, kd, vd, ko, vo, place[0] == 0, att_ref, put)
    picked = dot(so_ref[...], own_ref[...].astype(BF16))
    out_ref[:, wide:] = picked[:, wide:].astype(BF16)
    picked = picked[:, 0:wide] + dot(sp_ref[...], att_ref[...].astype(BF16))
    out_ref[:, 0:wide] = picked.astype(BF16)


def partner_specs(rows, wide):
    return [
        pl.BlockSpec((rows, wide), lambda i, t: (0, 0)),
        pl.BlockSpec((rows, 2 * HD), lambda i, t: (0, 0)),
        pl.BlockSpec((rows, 2 * HD), lambda i, t: (0, 1)),
        pl.BlockSpec((rows, 2 * HD), lambda i, t: (0, t[0])),
        pl.BlockSpec((rows, 2 * HD), lambda i, t: (0, t[0])),
    ]


def attend_partner_a(place, query_a, partner_kv, key_rows, value_rows, att_own, picks):
    rows, wide = query_a.shape
    half = att_own.shape[1]
    return pl.pallas_call(
        partner_a_kernel,
        grid_spec=pltpu.PrefetchScalarGridSpec(
            num_scalar_prefetch=1,
            grid=(1,),
            in_specs=partner_specs(rows, wide)
            + [
                pl.BlockSpec((rows, half), lambda i, t: (0, 0)),
                pl.BlockSpec((EARLY_ROWS, rows), lambda i, t: (0, t[0])),
                pl.BlockSpec((EARLY_ROWS, rows), lambda i, t: (0, 1 - t[0])),
            ],
            out_specs=[
                pl.BlockSpec((rows, wide), lambda i, t: (0, 0)),
                pl.BlockSpec((rows, HD), lambda i, t: (0, 0)),
                pl.BlockSpec((EARLY_ROWS, half), lambda i, t: (0, 0)),
            ],
        ),
        out_shape=[
            jax.ShapeDtypeStruct((rows, wide), F32),
            jax.ShapeDtypeStruct((rows, HD), F32),
            jax.ShapeDtypeStruct((EARLY_ROWS, half), BF16),
        ],
        name="attend_partner_a",
    )(place, query_a, partner_kv, partner_kv, key_rows, value_rows, att_own, picks, picks)


def partner_b_kernel(place, q_ref, kd, vd, ko, vo, sqo_ref, sqa_ref, so_ref, sp_ref, early_ref, *refs):
    att_ref, sum_ref = refs[0:2]
    out_refs, sq_ref = refs[2:-1], refs[-1]
    wide = early_ref.shape[1] - q_ref.shape[1]

    def put(squares):
        sq_ref[...] = sqa_ref[...] + squares

    first = H // 2 - q_ref.shape[1] // HD
    attend_heads(q_ref, first, kd, vd, ko, vo, place[0] == 0, att_ref, put)
    absent = absent_of(so_ref[...], sp_ref[...])
    picked = dot(sp_ref[...], att_ref[...].astype(BF16)) + early_ref[:, wide:].astype(F32)
    picked = (picked + absent).astype(BF16)
    early = (early_ref[:, 0:wide].astype(F32) + absent).astype(BF16)
    for index, out_ref in enumerate(out_refs):
        at = slice(index * ROWS, (index + 1) * ROWS)
        out_ref[:, 0:wide] = early[at]
        out_ref[:, wide:] = picked[at]
    ones = jnp.ones((8, HD), F32)

    def lanes(values):
        return lax.dot_general(
            ones,
            values,
            (((1,), (1,)), ((), ())),
            precision=lax.Precision.HIGHEST,
            preferred_element_type=F32,
        )

    sum_ref[0:8, :] = lanes(sq_ref[...])
    sum_ref[8:16, :] = lanes(sqo_ref[0] + sqo_ref[1])


def attend_partner_b(
    place, query_b, partner_kv, key_rows, value_rows, sq_own, sq_a, picks, early_a
):
    rows, wide = query_b.shape
    half = early_a.shape[1]
    whole = lambda i, t: (0, 0)
    return pl.pallas_call(
        partner_b_kernel,
        grid_spec=pltpu.PrefetchScalarGridSpec(
            num_scalar_prefetch=1,
            grid=(1,),
            in_specs=partner_specs(rows, wide)
            + [
                pl.BlockSpec((2, rows, HD), lambda i, t: (0, 0, 0)),
                pl.BlockSpec((rows, HD), whole),
                pl.BlockSpec((EARLY_ROWS, rows), lambda i, t: (0, t[0])),
                pl.BlockSpec((EARLY_ROWS, rows), lambda i, t: (0, 1 - t[0])),
                pl.BlockSpec((EARLY_ROWS, half), whole),
            ],
            out_specs=[
                pl.BlockSpec((rows, wide), whole),
                pl.BlockSpec((16, rows), whole),
            ]
            + [pl.BlockSpec((ROWS, half), whole)] * len(EARLY),
            scratch_shapes=[pltpu.VMEM((rows, HD), F32)],
        ),
        out_shape=[
            jax.ShapeDtypeStruct((rows, wide), F32),
            jax.ShapeDtypeStruct((16, rows), F32),
        ]
        + [jax.ShapeDtypeStruct((ROWS, half), BF16)] * len(EARLY),
        name="attend_partner_b",
    )(
        place, query_b, partner_kv, partner_kv, key_rows, value_rows,
        sq_own, sq_a, picks, picks, early_a,
    )


def row_scale(first, second):
    total = lax.dot_general(
        first + second,
        jnp.full((8, HD), 0.125, F32),
        (((0,), (0,)), ((), ())),
        precision=lax.Precision.HIGHEST,
        preferred_element_type=F32,
    )
    return lax.rsqrt(total * (1.0 / D) + EPSILON)[:, 0:1]


def late_kernel(
    place, own_ref, pa_ref, pb_ref, mine_ref, theirs_ref, gain_ref, so_ref, sp_ref,
    stay_ref, leave_ref, first_ref, second_ref,
):
    wide = pa_ref.shape[1]
    own_scale = row_scale(mine_ref[8:16, :], theirs_ref[0:8, :])
    other_scale = row_scale(mine_ref[0:8, :], theirs_ref[8:16, :])
    gain = gain_ref[...]
    first_ref[...] = (own_ref[...] * own_scale * gain).astype(BF16)
    second_ref[:, 0:wide] = (pa_ref[...] * other_scale * gain[:, 0:wide]).astype(BF16)
    second_ref[:, wide:] = (pb_ref[...] * other_scale * gain[:, wide:]).astype(BF16)
    first, second = so_ref[EARLY_ROWS:, :], sp_ref[EARLY_ROWS:, :]
    picked = dot(first, first_ref[...]) + dot(second, second_ref[...])
    picked = (picked + absent_of(first, second)).astype(BF16)
    stay_ref[...] = picked[0:LATE_ROWS]
    leave_ref[...] = picked[LATE_ROWS:]


def late_rows(place, att_own, att_a, att_b, mine, theirs, norm_gain, picks):
    rows, half = att_own.shape
    wide, last = att_a.shape[1], att_b.shape[1]
    all_rows = picks.shape[0]
    whole = lambda i, t: (0, 0)
    return pl.pallas_call(
        late_kernel,
        grid_spec=pltpu.PrefetchScalarGridSpec(
            num_scalar_prefetch=1,
            grid=(1,),
            in_specs=[
                pl.BlockSpec((rows, half), whole),
                pl.BlockSpec((rows, wide), whole),
                pl.BlockSpec((rows, last), whole),
                pl.BlockSpec((16, rows), whole),
                pl.BlockSpec((16, rows), whole),
                pl.BlockSpec((1, half), lambda i, t: (0, t[0])),
                pl.BlockSpec((all_rows, rows), lambda i, t: (0, t[0])),
                pl.BlockSpec((all_rows, rows), lambda i, t: (0, 1 - t[0])),
            ],
            out_specs=[pl.BlockSpec((LATE_ROWS, half), whole)] * 2,
            scratch_shapes=[pltpu.VMEM((rows, half), BF16)] * 2,
        ),
        out_shape=[jax.ShapeDtypeStruct((LATE_ROWS, half), BF16)] * 2,
        name="late_rows",
    )(place, att_own, att_a, att_b, mine, theirs, norm_gain, picks, picks)


def harvest_kernel(place, own_ref, pa_ref, pb_ref, mine_ref, theirs_ref, gain_ref, out_ref):
    wide = pa_ref.shape[1]
    gain = gain_ref[...]

    @pl.when(pl.program_id(0) == place[0])
    def _():
        scale = row_scale(mine_ref[8:16, :], theirs_ref[0:8, :])
        out_ref[...] = (own_ref[...] * scale * gain).astype(BF16)

    @pl.when(pl.program_id(0) != place[0])
    def _():
        scale = row_scale(mine_ref[0:8, :], theirs_ref[8:16, :])
        out_ref[:, 0:wide] = (pa_ref[...] * scale * gain[:, 0:wide]).astype(BF16)
        out_ref[:, wide:] = (pb_ref[...] * scale * gain[:, wide:]).astype(BF16)


def harvest_rows(place, att_own, att_a, att_b, mine, theirs, norm_gain):
    rows, half = att_own.shape
    whole = lambda i, t: (0, 0)
    return pl.pallas_call(
        harvest_kernel,
        grid_spec=pltpu.PrefetchScalarGridSpec(
            num_scalar_prefetch=1,
            grid=(2,),
            in_specs=[
                pl.BlockSpec(att_own.shape, whole),
                pl.BlockSpec(att_a.shape, whole),
                pl.BlockSpec(att_b.shape, whole),
                pl.BlockSpec((16, rows), whole),
                pl.BlockSpec((16, rows), whole),
                pl.BlockSpec((1, half), lambda i, t: (0, t[0])),
            ],
            out_specs=pl.BlockSpec((rows, half), lambda i, t: (i, 0)),
        ),
        out_shape=jax.ShapeDtypeStruct((2 * rows, half), BF16),
        name="harvest_rows",
    )(place, att_own, att_a, att_b, mine, theirs, norm_gain)


def picks_kernel(col_ref, row_ref, key_ref, out_ref):
    tokens = row_ref.shape[1]
    label = row_ref[...]
    before = lax.broadcasted_iota(jnp.int32, (tokens, tokens), 0)
    at = lax.broadcasted_iota(jnp.int32, (tokens, tokens), 1)
    same = jnp.logical_and(col_ref[...] == label, before < at)
    rank = jnp.sum(jnp.where(same, 1, 0), axis=0, keepdims=True)
    token_key = jnp.where(jnp.logical_and(label < C, rank < 16), label * 16 + rank, -1)
    out_ref[...] = jnp.where(key_ref[...] == token_key, 1.0, 0.0).astype(BF16)


def class_picks(labels, classes):
    tokens = labels.shape[0]
    slots = jnp.arange(SLOT, dtype=jnp.int32)
    keys = (classes[:, :, None] * 16 + slots[None, None, :]).reshape(-1, 1)
    return pl.pallas_call(
        picks_kernel,
        in_specs=[VMEM_SPEC] * 3,
        out_specs=VMEM_SPEC,
        out_shape=jax.ShapeDtypeStruct((keys.shape[0], tokens), BF16),
        name="class_picks",
    )(labels.reshape(tokens, 1), labels.reshape(1, tokens), keys)


def present_of(rows):
    return rows[:, 0:1].astype(F32) < 0.5 * ABSENT


def scale_kernel(place, *refs):
    own_refs, other_refs = refs[0:PAIRS], refs[PAIRS : 2 * PAIRS]
    gain_ref, other_gain_ref, own_out, other_out, flag_ref = refs[2 * PAIRS :]
    for piece in range(PAIRS):
        at = slice(piece * SPAN, (piece + 1) * SPAN)
        present = present_of(own_refs[piece])
        rows = jnp.where(present, own_refs[piece][...].astype(F32), 0.0)
        other = jnp.where(present, other_refs[piece][...].astype(F32), 0.0)
        squares = jnp.sum(rows * rows + other * other, axis=-1, keepdims=True)
        scale = lax.rsqrt(squares * (1.0 / D) + EPSILON)
        own_out[at, :] = (rows * scale * gain_ref[...]).astype(BF16)
        other_out[at, :] = (other * scale * other_gain_ref[...]).astype(BF16)
        flag_ref[at, :] = jnp.broadcast_to(jnp.where(present, 1.0, 0.0), (SPAN, HD))


def scale_early(place, own, other, norm_gain):
    half = own[0].shape[1]
    whole = lambda i, t: (0, 0)
    return pl.pallas_call(
        scale_kernel,
        grid_spec=pltpu.PrefetchScalarGridSpec(
            num_scalar_prefetch=1,
            grid=(1,),
            in_specs=[pl.BlockSpec((SPAN, half), whole)] * (2 * PAIRS)
            + [
                pl.BlockSpec((1, half), lambda i, t: (0, t[0])),
                pl.BlockSpec((1, half), lambda i, t: (0, 1 - t[0])),
            ],
            out_specs=[pl.BlockSpec((EARLY_ROWS, half), whole)] * 2
            + [pl.BlockSpec((EARLY_ROWS, HD), whole)],
        ),
        out_shape=[jax.ShapeDtypeStruct((EARLY_ROWS, half), BF16)] * 2
        + [jax.ShapeDtypeStruct((EARLY_ROWS, HD), F32)],
        name="scale_early",
    )(place, *own, *other, norm_gain, norm_gain)


def tdot(left, right):
    return lax.dot_general(left, right, (((0,), (0,)), ((), ())), preferred_element_type=F32)


def gram_own_kernel(place, *refs):
    early_ref, early_flag_ref = refs[0:2]
    late_refs = refs[2 : 2 + len(LATE)]
    out_ref, rows_ref, flag_ref = refs[2 + len(LATE) :]
    step = out_ref.shape[0]

    @pl.when(pl.program_id(0) == 0)
    def _():
        rows_ref[0:EARLY_ROWS, :] = early_ref[...]
        flag_ref[0:EARLY_ROWS, :] = early_flag_ref[...]
        for piece in range(len(LATE)):
            at = slice(EARLY_ROWS + piece * SPAN, EARLY_ROWS + (piece + 1) * SPAN)
            present = present_of(late_refs[piece])
            rows_ref[at, :] = jnp.where(present, late_refs[piece][...].astype(F32), 0.0).astype(BF16)
            flag_ref[at, :] = jnp.broadcast_to(jnp.where(present, 1.0, 0.0), (SPAN, HD))

    count = jnp.sum(flag_ref[:, 0:1])
    left = rows_ref[:, pl.ds(pl.multiple_of(pl.program_id(0) * step, step), step)]
    out_ref[...] = (tdot(left, rows_ref[...]) * (1.0 / count)).astype(BF16)


def gram_own(place, early, early_flags, late):
    half = early.shape[1]
    total = PIECES * SPAN
    step = 512
    whole = lambda i, t: (0, 0)
    return pl.pallas_call(
        gram_own_kernel,
        grid_spec=pltpu.PrefetchScalarGridSpec(
            num_scalar_prefetch=1,
            grid=(half // step,),
            in_specs=[
                pl.BlockSpec((EARLY_ROWS, half), whole),
                pl.BlockSpec((EARLY_ROWS, HD), whole),
            ]
            + [pl.BlockSpec((SPAN, half), whole)] * len(LATE),
            out_specs=[
                pl.BlockSpec((step, half), lambda i, t: (i, t[0])),
                pl.BlockSpec((total, half), whole),
                pl.BlockSpec((total, HD), whole),
            ],
        ),
        out_shape=[
            jax.ShapeDtypeStruct((half, 2 * half), BF16),
            jax.ShapeDtypeStruct((total, half), BF16),
            jax.ShapeDtypeStruct((total, HD), F32),
        ],
        name="gram_own",
    )(place, early, early_flags, *late)


def gram_other_kernel(place, *refs):
    early_ref = refs[0]
    late_refs = refs[1 : 1 + len(LATE)]
    left_ref, flag_ref, _, out_ref, rows_ref = refs[1 + len(LATE) :]

    @pl.when(pl.program_id(0) == 0)
    def _():
        rows_ref[0:EARLY_ROWS, :] = early_ref[...]
        for piece in range(len(LATE)):
            at = slice(EARLY_ROWS + piece * SPAN, EARLY_ROWS + (piece + 1) * SPAN)
            present = flag_ref[at, 0:1] > 0.5
            rows_ref[at, :] = jnp.where(present, late_refs[piece][...].astype(F32), 0.0).astype(BF16)

    count = jnp.sum(flag_ref[:, 0:1])
    out_ref[...] = (tdot(left_ref[...], rows_ref[...]) * (1.0 / count)).astype(BF16)


def gram_other(place, early, late, rows, flags, partial):
    half = early.shape[1]
    total = PIECES * SPAN
    step = 512
    whole = lambda i, t: (0, 0)
    return pl.pallas_call(
        gram_other_kernel,
        grid_spec=pltpu.PrefetchScalarGridSpec(
            num_scalar_prefetch=1,
            grid=(half // step,),
            in_specs=[pl.BlockSpec((EARLY_ROWS, half), whole)]
            + [pl.BlockSpec((SPAN, half), whole)] * len(LATE)
            + [
                pl.BlockSpec((total, step), lambda i, t: (0, i)),
                pl.BlockSpec((total, HD), whole),
                pl.BlockSpec(memory_space=pl.ANY),
            ],
            out_specs=pl.BlockSpec((step, half), lambda i, t: (i, 1 - t[0])),
            scratch_shapes=[pltpu.VMEM((total, half), BF16)],
        ),
        out_shape=jax.ShapeDtypeStruct((half, 2 * half), BF16),
        input_output_aliases={len(LATE) + 4: 0},
        name="gram_other",
    )(place, early, *late, rows, flags, partial)


def after(value, *earlier):
    return lax.optimization_barrier((value, *earlier))[0]


def paired_local(queries, key_rows, value_rows, norm_gain, labels, pair_list, owner_map):
    group_count = lax.axis_size("dp")
    my_tensor = lax.axis_index("tensor")
    my_group = lax.axis_index("dp")
    place = jnp.full((1,), my_tensor, jnp.int32)
    swap = [(0, 1), (1, 0)]

    def across(value, name):
        with jax.named_scope(name):
            return lax.ppermute(value, "tensor", swap)

    def hop(value, offset, name):
        with jax.named_scope(name):
            return lax.ppermute(value, "dp", [(i, i ^ offset) for i in range(group_count)])

    def theirs(rows, start, width):
        return lax.dynamic_slice_in_dim(rows, (1 - my_tensor) * start, width, 1)

    part = 2 * HD
    sent_kv = jnp.concatenate([theirs(key_rows, part, part), theirs(value_rows, part, part)], 1)
    partner_kv = across(sent_kv, "x_kv")
    other_half = (1 - my_tensor) * (D // 2)
    last = D // 2 - WIDE_A
    sent_a = lax.dynamic_slice_in_dim(queries, other_half, WIDE_A, 1)
    sent_b = lax.dynamic_slice_in_dim(queries, other_half + WIDE_A, last, 1)
    query_a = across(sent_a, "x_qa")
    query_b = across(after(sent_b, partner_kv), "x_qb")

    order = jnp.asarray(EARLY + LATE + tuple(j + 1 for j in LATE), jnp.int32)
    classes = pair_list[owner_map[my_group ^ order]]
    picks = class_picks(labels, classes)
    gain = norm_gain.reshape(1, D)

    att_own, sq_own = attend_own(place, queries, key_rows, value_rows, partner_kv)
    att_a, sq_a, early_a = attend_partner_a(
        place, query_a, partner_kv, key_rows, value_rows, att_own, picks
    )
    att_b, mine, *early = attend_partner_b(
        place, query_b, partner_kv, key_rows, value_rows, sq_own, sq_a, picks, early_a
    )
    early = dict(zip(EARLY, early))
    came, own, other, crossed = {0: early[0]}, {}, {}, []

    def send_early(j, *earlier):
        came[j] = hop(after(early[j], *earlier), j, f"far_e{j}")

    def send_late(j, *earlier):
        own[j] = hop(after(joined[j], *earlier), j, f"far_{j}")

    def cross(j, *earlier):
        other[j] = across(after(own[j], *earlier, *crossed[-2:-1]), f"x_{j}")
        crossed.append(other[j])

    for j in (8, 12, 1, 2):
        send_early(j)
    sums = across(mine, "x_sums")
    send_early(3, came[2])
    send_early(9, came[1])
    own[0] = jnp.concatenate([came[0], came[1]])
    cross(0)
    ready = after(sums, came[1], came[2])
    stay, leave = late_rows(place, att_own, att_a, att_b, mine, ready, gain, picks)
    send_early(13, leave)
    swapped = hop(after(leave, came[3], came[8], other[0]), 1, "far_core")
    shape = (len(LATE), ROWS, D // 2)
    joined = jnp.concatenate([stay.reshape(shape), swapped.reshape(shape)], 1)
    joined = {j: joined[index] for index, j in enumerate(LATE)}
    own[2] = jnp.concatenate([came[2], came[3]])
    cross(2)
    send_late(10, came[12])
    own[8] = jnp.concatenate([came[8], came[9]])
    cross(8)
    send_late(14, came[9], other[2])
    send_late(4, came[13], other[2])
    own[12] = jnp.concatenate([came[12], came[13]])
    cross(12)
    send_late(6, own[4], other[8])
    cross(4)
    harvest = harvest_rows(place, att_own, att_a, att_b, mine, ready, gain)
    cross(10, harvest)
    cross(6)
    pairs = EARLY[0::2]
    own_early, other_early, early_flags = scale_early(
        place, [own[j] for j in pairs], [other[j] for j in pairs], gain
    )
    cross(14, own_early)
    partial, rows, flags = gram_own(place, own_early, early_flags, [own[j] for j in LATE])
    gram = gram_other(
        place, other_early, [other[j] for j in LATE], rows, flags, partial
    )
    return gram[None], harvest


def solution(mesh):
    paired = mesh.shape["tensor"] == 2 and mesh.shape["dp"] == P_SIZE
    return jax.shard_map(
        paired_local if paired else general_local,
        mesh=mesh,
        in_specs=(
            P(("dp", "tensor"), None),
            P(("dp", "tensor"), None),
            P(("dp", "tensor"), None),
            P(),
            P("dp"),
            P(),
            P(),
        ),
        out_specs=(P("dp", "tensor", None), P("dp", "tensor")),
        check_vma=False,
    )
```
